1024 devices in a mesh: tm: 16 (over x, core), seq: 8 (over y), mp: 8 (over z).
Axes of the slice: x: 8, y: 8, z: 8, core: 2. Of those that a mesh axis runs over, the one named last changes fastest.
Arguments:
- student_q: bfloat16 [8, 2048, 5120], P('seq', 'tm', 'mp'), may hold values from -110 to 110
- student_k: bfloat16 [8, 2048, 5120], P('seq', 'tm', 'mp'), may hold values from -6 to 6
- student_v: bfloat16 [8, 2048, 5120], P('seq', 'tm', 'mp'), may hold values from -6 to 6
- teacher_q: bfloat16 [8, 2048, 5120], P('seq', 'tm', 'mp'), may hold values from -110 to 110
- teacher_k: bfloat16 [8, 2048, 5120], P('seq', 'tm', 'mp'), may hold values from -6 to 6
- stagger: int32 [8], P('seq'), may hold values from 0 to 8, as said below
- clip_lengths: int32 [8, 3], P('seq'), may hold values from 1 to 9, 16 in all within a row
Outputs:
- generated: bfloat16 [8, 2048, 5120], P('seq', 'tm', 'mp')
- score_rows: bfloat16 [8, 2048, 5120], P('seq', 'tm', 'mp')
The draws below stay inside these ranges and needn't reach their ends.
Inputs may be any that keep to these rules, and one draw needn't show every extreme that they name: `clip_lengths`: the lengths of each video sum to 16, and some clip has 9 blocks. `stagger`: some video has the value 16 // 2.
All inputs are finite; a program needn't handle non-finite values.
Results may differ from the reference program's by a relative error of at most 0.007.
Values may be sent and summed in bfloat16 or wider, within the bound.
A program may use at most 32 MiB of HBM per device.

```python
import math
import jax
import jax.numpy as jnp
import numpy as np
from jax import lax

HEADS = 40
HD = 128
TOK = 128
CLIPS = 3
BLOCKS = 16
VIDEOS = 8
F = 5120


def pair_draw(key, salt):
    base = jax.random.fold_in(key, salt)
    query_key, key_key = jax.random.split(base)
    shape = (VIDEOS, BLOCKS * TOK, HEADS * HD)
    queries = jnp.clip(jax.random.normal(query_key, shape, jnp.float32), -6.0, 6.0)
    keys = jnp.clip(jax.random.normal(key_key, shape, jnp.float32), -6.0, 6.0)
    return (queries, keys)


def draw_student_q(key, part):
    return pair_draw(key, 11)[0].astype(jnp.bfloat16)


def draw_student_k(key, part):
    return pair_draw(key, 11)[1].astype(jnp.bfloat16)


def draw_teacher_q(key, part):
    return pair_draw(key, 23)[0].astype(jnp.bfloat16)


def draw_teacher_k(key, part):
    return pair_draw(key, 23)[1].astype(jnp.bfloat16)


def draw_stagger(key, part):
    value_key, place_key = jax.random.split(jax.random.fold_in(key, 37))
    values = jax.random.randint(value_key, (VIDEOS,), 0, BLOCKS // 2 + 1).astype(jnp.int32)
    place = jax.random.randint(place_key, (), 0, VIDEOS).astype(jnp.int32)
    return jnp.where(jnp.arange(VIDEOS, dtype=jnp.int32) == place, jnp.int32(BLOCKS // 2), values).astype(jnp.int32)


def steps_of(stream_key, extent, cuts, low, largest):
    level = 1.0
    for axis_at, parts in cuts:
        steps = jax.random.uniform(jax.random.fold_in(jax.random.fold_in(stream_key, 6), axis_at), (parts,), jnp.float32, low / len(cuts), largest / len(cuts))
        level = level * jnp.repeat(jnp.exp(steps), extent[axis_at] // parts).reshape((-1,) + (1,) * (len(extent) - 1 - axis_at))
    return level


def split_up(number_of, total, reach, lean):
    portions = [(1 << 20) // math.isqrt(rank ** lean) + 1 for rank in range(2, number_of + 1)]
    surplus, counts = total - reach - (number_of - 1), [1] * (number_of - 1)
    while surplus > 0:
        free = [i for i in range(number_of - 1) if counts[i] < reach]
        whole, budget = sum([portions[i] for i in free]), surplus
        for i in free:
            more = min(reach - counts[i], max(1, budget * portions[i] // whole), surplus)
            counts[i] = counts[i] + more
            surplus = surplus - more
    return np.array([reach] + counts)


def ragged_sizes(stream_key, count, total, limit, skew):
    if count == 2:
        one = jax.random.randint(stream_key, (), max(1, total - limit), min(limit, total - 1) + 1)
        return jnp.stack([one, total - one])
    lengths = jnp.asarray(split_up(count, total, limit, skew), jnp.int32)
    couples = (count - 1) // 2
    giver, sink = lengths[1:1 + 2 * couples:2], lengths[2:2 + 2 * couples:2]
    margin = jnp.minimum(giver - 1, limit - sink)
    moved = jax.random.randint(jax.random.fold_in(stream_key, 1), (couples,), 0, 1 << 20) % (margin + 1)
    lengths = lengths.at[1:1 + 2 * couples:2].set(giver - moved).at[2:2 + 2 * couples:2].set(sink + moved)
    return lengths[jax.random.permutation(jax.random.fold_in(stream_key, 2), count)]


def centred(rng, shape, deviation, limit, pieces=(), kind=jnp.bfloat16):
    entries = jax.random.normal(rng, shape, jnp.float32) * deviation
    if len(pieces) > 0:
        entries = steps_of(rng, shape, pieces, -0.22, 0.18) * entries
    return jnp.clip(entries, min=-limit, max=limit).astype(kind)


def setup_inputs(seed: int = 0) -> dict:
    key_list = jax.random.split(jax.random.key(seed), 8)
    return {
        "student_q": draw_student_q(jax.random.fold_in(key_list[7], 71), 0),
        "student_k": draw_student_k(jax.random.fold_in(key_list[7], 71), 0),
        "student_v": centred(key_list[2], (VIDEOS, BLOCKS * TOK, F), 1.0, 6.0, ((0, 8), (1, 16), (2, 8))),
        "teacher_q": draw_teacher_q(jax.random.fold_in(key_list[7], 71), 0),
        "teacher_k": draw_teacher_k(jax.random.fold_in(key_list[7], 71), 0),
        "stagger": draw_stagger(jax.random.fold_in(key_list[7], 71), 0),
        "clip_lengths": jax.vmap(lambda own: ragged_sizes(own, CLIPS, BLOCKS, BLOCKS // 2 + 1, 0))(jax.random.split(key_list[6], VIDEOS)).reshape((VIDEOS, CLIPS)).astype(jnp.int32),
    }


negative = -1e+30

def attend_rule(queries, keys, values, allowed):
    rows = queries.shape[0]
    qh = queries.astype(jnp.float32).reshape(rows, HEADS, HD)
    kh = keys.astype(jnp.float32).reshape(rows, HEADS, HD)
    vh = values.astype(jnp.float32).reshape(rows, HEADS, HD)
    scores = jnp.einsum('qhd,khd->hqk', qh, kh) / math.sqrt(HD)
    scores = jnp.where(allowed[None], scores, negative)
    top = lax.optimization_barrier(jnp.max(scores, axis=-1))
    weights = jnp.where(allowed[None], jnp.exp(scores - top[..., None]), 0.0)
    total = lax.optimization_barrier(jnp.sum(weights, axis=-1))
    rounded = weights.astype(jnp.bfloat16).astype(jnp.float32)
    mixed = jnp.einsum('hqk,khd->qhd', rounded, vh)
    mixed = mixed / jnp.transpose(total)[..., None]
    return mixed.reshape(rows, HEADS * HD)

def one_video(packed_tokens):
    student_query_rows, student_key_rows, student_value_rows, teacher_query_rows, teacher_key_rows, opening_block, clip_length_list = packed_tokens
    block = (jnp.arange(BLOCKS * TOK) // TOK).astype(jnp.int32)
    student_block_mask = (block[None, :] == block[:, None]) | (block[None, :] >= opening_block) & (block[None, :] < block[:, None])
    generated = attend_rule(student_query_rows, student_key_rows, student_value_rows, student_block_mask).astype(jnp.bfloat16)
    running = jnp.cumsum(clip_length_list)
    clip = lax.optimization_barrier(jnp.sum((running[None, :] <= block[:, None]).astype(jnp.int32), axis=1))
    teacher_mask = clip[:, None] == clip[None, :]
    teacher_out = attend_rule(teacher_query_rows, teacher_key_rows, generated, teacher_mask)
    score_rows = (teacher_out - generated.astype(jnp.float32)).astype(jnp.bfloat16)
    return (generated, score_rows)

def reference(student_q, student_k, student_v, teacher_q, teacher_k, stagger, clip_lengths):
    return lax.map(one_video, (student_q, student_k, student_v, teacher_q, teacher_k, stagger, clip_lengths))
```

```python
import math

import jax
import jax.numpy as jnp
from jax import lax
from jax.experimental import pallas as pl
from jax.experimental.pallas import tpu as pltpu
from jax.sharding import PartitionSpec as P

HD = 128
TOK = 128
CHIPS = 8
HEADS = 5
BLOCKS = 16
MESH = pl.DeviceIdType.MESH
NEG = -1e30
FACTOR = math.log2(math.e) / math.sqrt(HD)
HOME = tuple(CHIPS * h // HEADS for h in range(HEADS))
ORDER = (0, 1, 7, 2, 6, 3, 5, 4)

Q, K, V, TQ, TK = range(5)
RELAYED = (K, V, TK)


def kernel(
    sq, sk, sv, tq, tk, stagger, clips, gen, score,
    qb, kb, vb, tqb, tkb, gb, sb, scores,
    send, recv, rel_send, rel_recv, gx_send, gx_recv, go_send, go_recv, so_send, so_recv,
):
    me = lax.axis_index("tm")
    x = me // 2
    c = lax.rem(me, 2)
    mine = (5 * x + 4) // CHIPS
    active = x == HOME[0]
    for h in range(1, HEADS):
        active = active | (x == HOME[h])
    inputs = (sq, sk, sv, tq, tk)
    buffers = (qb, kb, vb, tqb, tkb)
    other = {"tm": 2 * x + 1 - c}

    def rows(block):
        return pl.ds(pl.multiple_of(block * TOK, TOK), TOK)

    def head(h):
        return pl.ds(pl.multiple_of(h * HD, HD), HD)

    def place(a, chip, core):
        return buffers[a].at[rows(chip) if a in (Q, TQ) else rows(2 * chip + core)]

    barrier = pltpu.get_barrier_semaphore()
    for h in range(HEADS):
        @pl.when(x != HOME[h])
        def _():
            pl.semaphore_signal(barrier, inc=1, device_id={"tm": 2 * HOME[h] + c}, device_id_type=MESH)

    @pl.when(active)
    def _():
        for idle in range(CHIPS):
            if idle not in HOME:
                pl.semaphore_signal(barrier, inc=1, device_id={"tm": 2 * idle + c}, device_id_type=MESH)
        pl.semaphore_signal(barrier, inc=1, device_id=other, device_id_type=MESH)
        pl.semaphore_wait(barrier, CHIPS)

    @pl.when(jnp.logical_not(active))
    def _():
        pl.semaphore_wait(barrier, HEADS)

    def outgoing(a, h):
        return pltpu.make_async_remote_copy(
            src_ref=inputs[a].at[0, :, pl.ds(h * HD, HD)],
            dst_ref=place(a, x, c),
            send_sem=send.at[a, h],
            recv_sem=recv.at[a, x],
            device_id={"tm": 2 * HOME[h] + c},
            device_id_type=MESH,
        )

    for a in (K, Q, V, TQ, TK):
        for h in range(HEADS):
            @pl.when(x != HOME[h])
            def _():
                outgoing(a, h).start()

            @pl.when(x == HOME[h])
            def _():
                pltpu.make_async_copy(
                    inputs[a].at[0, :, pl.ds(h * HD, HD)], place(a, x, c), recv.at[a, x]
                ).start()

    def arrived(a, chip):
        pltpu.make_async_copy(place(a, chip, c), place(a, chip, c), recv.at[a, chip]).wait()

    def relay(a, chip):
        r = RELAYED.index(a)
        return pltpu.make_async_remote_copy(
            src_ref=place(a, chip, c),
            dst_ref=place(a, chip, c),
            send_sem=rel_send.at[r, chip],
            recv_sem=rel_recv.at[r, chip],
            device_id=other,
            device_id_type=MESH,
        )

    def relayed(a, chip):
        r = RELAYED.index(a)
        pltpu.make_async_copy(place(a, chip, 1 - c), place(a, chip, 1 - c), rel_recv.at[r, chip]).wait()

    def to_other(i):
        return pltpu.make_async_remote_copy(
            src_ref=gb.at[rows(2 * i + c)],
            dst_ref=gb.at[rows(2 * i + c)],
            send_sem=gx_send.at[i],
            recv_sem=gx_recv.at[i],
            device_id=other,
            device_id_type=MESH,
        )

    def to_owner(i, source, target, sends, recvs):
        return pltpu.make_async_remote_copy(
            src_ref=source,
            dst_ref=target.at[0, :, head(mine)],
            send_sem=sends.at[i],
            recv_sem=recvs.at[mine],
            device_id={"tm": 2 * i + c},
            device_id_type=MESH,
        )

    def hand_over(i, source, target, sends, recvs):
        @pl.when(x != i)
        def _():
            to_owner(i, source, target, sends, recvs).start()

        @pl.when(x == i)
        def _():
            pltpu.make_async_copy(source, target.at[0, :, head(mine)], recvs.at[mine]).start()

    def generated(i):
        return gb.at[rows(2 * i + c)]

    def scored(i):
        return sb.at[pl.ds(i * TOK, TOK)]

    def attend(queries, keys, values, tiles, bias):
        top = [None, None]
        for t in tiles:
            s = lax.dot_general(
                queries, keys[t * 256 : t * 256 + 256, :], (((1,), (1,)), ((), ())),
                preferred_element_type=jnp.float32,
            )
            for r in range(2):
                for u in range(2):
                    piece = s[r * TOK : r * TOK + TOK, u * TOK : u * TOK + TOK] + bias(r, 2 * t + u)
                    scores[r * TOK : r * TOK + TOK, (2 * t + u) * TOK : (2 * t + u + 1) * TOK] = piece
                    top[r] = piece if top[r] is None else jnp.maximum(top[r], piece)
        peak = jnp.concatenate([jnp.max(top[r], axis=1, keepdims=True) for r in range(2)], axis=0)
        total = jnp.zeros((2 * TOK, TOK), jnp.float32)
        acc = jnp.zeros((2 * TOK, HD), jnp.float32)
        for t in tiles:
            p = jnp.exp2((scores[:, t * 256 : t * 256 + 256] - peak) * FACTOR)
            total = total + (p[:, :TOK] + p[:, TOK:])
            acc = acc + jnp.dot(
                p.astype(jnp.bfloat16), values[t * 256 : t * 256 + 256, :],
                preferred_element_type=jnp.float32,
            )
        return acc / jnp.sum(total, axis=1, keepdims=True)

    @pl.when(active)
    def _():
        for d in ORDER:
            chip = lax.rem(x + d, CHIPS)
            for a in (K, Q, V):
                arrived(a, chip)
                if a in RELAYED:
                    relay(a, chip).start()
        for chip in range(CHIPS):
            relayed(K, chip)
            relayed(V, chip)

        first = stagger[0]
        for p in range(4):
            def student_bias(r, j):
                own = 2 * (2 * p + r) + c
                allowed = (j == own) | ((j >= first) & (j < own))
                return jnp.where(allowed, 0.0, NEG).astype(jnp.float32)

            mixed = attend(qb[p * 256 : p * 256 + 256, :], kb, vb, range(2 * p + 2), student_bias)
            mixed = mixed.astype(jnp.bfloat16)
            for r in range(2):
                gb[rows(2 * (2 * p + r) + c), :] = mixed[r * TOK : r * TOK + TOK, :]
            if p > 0:
                for i in (2 * p - 2, 2 * p - 1):
                    to_other(i).start()
                    hand_over(i, generated(i), gen, go_send, go_recv)

        for d in ORDER:
            chip = lax.rem(x + d, CHIPS)
            arrived(TQ, chip)
            arrived(TK, chip)
            relay(TK, chip).start()
            if d == 0:
                for i in (6, 7):
                    to_other(i).start()
                    hand_over(i, generated(i), gen, go_send, go_recv)
        for chip in range(CHIPS):
            relayed(TK, chip)
        for i in range(CHIPS):
            pltpu.make_async_copy(gb.at[rows(2 * i + 1 - c)], gb.at[rows(2 * i + 1 - c)], gx_recv.at[i]).wait()

        ends = [clips[0, 0], clips[0, 0] + clips[0, 1]]

        def clip_of(block):
            return (ends[0] <= block).astype(jnp.int32) + (ends[1] <= block).astype(jnp.int32)

        for p in range(4):
            def teacher_bias(r, j):
                same = clip_of(2 * (2 * p + r) + c) == clip_of(jnp.int32(j))
                return jnp.where(same, 0.0, NEG).astype(jnp.float32)

            tiles = range(max(0, 2 * p - 4), min(8, 2 * p + 6))
            mixed = attend(tqb[p * 256 : p * 256 + 256, :], tkb, gb, tiles, teacher_bias)
            for r in range(2):
                i = 2 * p + r
                own = gb[rows(2 * i + c), :].astype(jnp.float32)
                sb[i * TOK : i * TOK + TOK, :] = (mixed[r * TOK : r * TOK + TOK, :] - own).astype(jnp.bfloat16)
            if p > 0:
                for i in (2 * p - 2, 2 * p - 1):
                    hand_over(i, scored(i), score, so_send, so_recv)
        for i in (6, 7):
            hand_over(i, scored(i), score, so_send, so_recv)

        for chip in range(CHIPS):
            for a in RELAYED:
                relay(a, chip).wait_send()
            to_other(chip).wait_send()

            @pl.when(x != chip)
            def _():
                to_owner(chip, generated(chip), gen, go_send, go_recv).wait_send()
                to_owner(chip, scored(chip), score, so_send, so_recv).wait_send()

    for a in range(5):
        for h in range(HEADS):
            @pl.when(x != HOME[h])
            def _():
                outgoing(a, h).wait_send()

    for target, recvs in ((gen, go_recv), (score, so_recv)):
        for h in range(HEADS):
            spot = target.at[0, :, pl.ds(h * HD, HD)]
            pltpu.make_async_copy(spot, spot, recvs.at[h]).wait()


def per_device(student_q, student_k, student_v, teacher_q, teacher_k, stagger, clip_lengths):
    whole = jax.ShapeDtypeStruct(student_q.shape, jnp.bfloat16)
    anywhere = pl.BlockSpec(memory_space=pl.ANY)
    scalars = pl.BlockSpec(memory_space=pltpu.SMEM)
    half, full = (BLOCKS // 2 * TOK, HD), (BLOCKS * TOK, HD)
    dma = pltpu.SemaphoreType.DMA
    return pl.pallas_call(
        kernel,
        out_shape=(whole, whole),
        in_specs=[anywhere] * 5 + [scalars] * 2,
        out_specs=(anywhere, anywhere),
        scratch_shapes=[
            pltpu.VMEM(half, jnp.bfloat16),
            pltpu.VMEM(full, jnp.bfloat16),
            pltpu.VMEM(full, jnp.bfloat16),
            pltpu.VMEM(half, jnp.bfloat16),
            pltpu.VMEM(full, jnp.bfloat16),
            pltpu.VMEM(full, jnp.bfloat16),
            pltpu.VMEM(half, jnp.bfloat16),
            pltpu.VMEM((2 * TOK, BLOCKS * TOK), jnp.float32),
            dma((5, HEADS)),
            dma((5, CHIPS)),
            dma((3, CHIPS)),
            dma((3, CHIPS)),
            dma((CHIPS,)),
            dma((CHIPS,)),
            dma((CHIPS,)),
            dma((HEADS,)),
            dma((CHIPS,)),
            dma((HEADS,)),
        ],
        compiler_params=pltpu.CompilerParams(collective_id=0, has_side_effects=True),
        name="rollout",
    )(student_q, student_k, student_v, teacher_q, teacher_k, stagger, clip_lengths)


def solution(mesh):
    rows = P("seq", "tm", "mp")
    return jax.shard_map(
        per_device,
        mesh=mesh,
        in_specs=(rows,) * 5 + (P("seq"), P("seq", None)),
        out_specs=(rows, rows),
        check_vma=False,
    )
```

```python
import math

import jax
import jax.numpy as jnp
from jax import lax
from jax.experimental import pallas as pl
from jax.experimental.pallas import tpu as pltpu
from jax.sharding import PartitionSpec as P

HD = 128
TOK = 128
CHIPS = 8
HEADS = 5
BLOCKS = 16
MESH = pl.DeviceIdType.MESH
NEG = -1e30
FACTOR = math.log2(math.e) / math.sqrt(HD)
HOME = (0, 2, 3, 5, 6)
LATE = ((0,), (3, 5))
IDLE = tuple(chip for chip in range(CHIPS) if chip not in HOME)
ORDER = (0, 1, 7, 2, 6, 3, 5, 4)

Q, K, V, TQ, TK = range(5)
RELAYED = (K, V, TK)


def kernel(
    sq, sk, sv, tq, tk, stagger, clips, gen, score,
    qb, kb, vb, tqb, tkb, gb, sb, scores,
    send, recv, rel_send, rel_recv, gx_send, gx_recv, go_send, go_recv, so_send, so_recv, ready, settled,
):
    me = lax.axis_index("tm")
    x = me // 2
    c = lax.rem(me, 2)
    mine = sum(h * (x == HOME[h]).astype(jnp.int32) for h in range(HEADS))
    corner = (lax.axis_index("seq") == 0) & (lax.axis_index("mp") == 0)

    def late(h):
        return (corner & (HOME[h] in LATE[0])) | (jnp.logical_not(corner) & (HOME[h] in LATE[1]))

    lates = jnp.where(corner, len(LATE[0]), len(LATE[1]))
    active = x == HOME[0]
    last = (x == HOME[0]) & late(0)
    for h in range(1, HEADS):
        active = active | (x == HOME[h])
        last = last | ((x == HOME[h]) & late(h))
    inputs = (sq, sk, sv, tq, tk)
    buffers = (qb, kb, vb, tqb, tkb)
    other = {"tm": 2 * x + 1 - c}

    def rows(block):
        return pl.ds(pl.multiple_of(block * TOK, TOK), TOK)

    def head(h):
        return pl.ds(pl.multiple_of(h * HD, HD), HD)

    def place(a, chip, core):
        return buffers[a].at[rows(chip) if a in (Q, TQ) else rows(2 * chip + core)]

    barrier = pltpu.get_barrier_semaphore()
    early = active & jnp.logical_not(last)

    def greet(chip):
        pl.semaphore_signal(barrier, inc=1, device_id={"tm": 2 * chip + c}, device_id_type=MESH)

    @pl.when(early)
    def _():
        for d in ORDER[1:]:
            greet(lax.rem(x + d, CHIPS))

    @pl.when(jnp.logical_not(early))
    def _():
        for h in range(HEADS):
            @pl.when((x != HOME[h]) & late(h))
            def _():
                greet(HOME[h])

    @pl.when(active)
    def _():
        pl.semaphore_signal(barrier, inc=1, device_id=other, device_id_type=MESH)

    pl.semaphore_wait(barrier, jnp.where(last, CHIPS, HEADS - lates))

    @pl.when(last)
    def _():
        for chip in IDLE:
            pl.semaphore_signal(settled, inc=1, device_id={"tm": 2 * chip + c}, device_id_type=MESH)
        for h in range(HEADS):
            @pl.when(jnp.logical_not(late(h)))
            def _():
                pl.semaphore_signal(settled, inc=1, device_id={"tm": 2 * HOME[h] + c}, device_id_type=MESH)

    def outgoing(a, h):
        return pltpu.make_async_remote_copy(
            src_ref=inputs[a].at[0, :, pl.ds(h * HD, HD)],
            dst_ref=place(a, x, c),
            send_sem=send.at[a, h],
            recv_sem=recv.at[a, x],
            device_id={"tm": 2 * HOME[h] + c},
            device_id_type=MESH,
        )

    def submit(arrays, chosen):
        for a in arrays:
            for h in range(HEADS):
                @pl.when((x != HOME[h]) & chosen(h))
                def _():
                    outgoing(a, h).start()

                @pl.when((x == HOME[h]) & chosen(h))
                def _():
                    pltpu.make_async_copy(
                        inputs[a].at[0, :, pl.ds(h * HD, HD)], place(a, x, c), recv.at[a, x]
                    ).start()

    submit((K, Q, V), lambda h: jnp.logical_not(late(h)))

    @pl.when(jnp.logical_not(active))
    def _():
        for h in range(HEADS):
            @pl.when(jnp.logical_not(late(h)))
            def _():
                pl.semaphore_signal(ready, inc=1, device_id={"tm": 2 * HOME[h] + c}, device_id_type=MESH)

    @pl.when(jnp.logical_not(last))
    def _():
        pl.semaphore_wait(settled, lates)

    submit((K, Q, V), late)
    submit((TQ, TK), lambda h: True)

    def arrived(a, chip):
        pltpu.make_async_copy(place(a, chip, c), place(a, chip, c), recv.at[a, chip]).wait()

    def relay(a, chip):
        r = RELAYED.index(a)
        return pltpu.make_async_remote_copy(
            src_ref=place(a, chip, c),
            dst_ref=place(a, chip, c),
            send_sem=rel_send.at[r, chip],
            recv_sem=rel_recv.at[r, chip],
            device_id=other,
            device_id_type=MESH,
        )

    def relayed(a, chip):
        r = RELAYED.index(a)
        pltpu.make_async_copy(place(a, chip, 1 - c), place(a, chip, 1 - c), rel_recv.at[r, chip]).wait()

    def to_other(i):
        return pltpu.make_async_remote_copy(
            src_ref=gb.at[rows(2 * i + c)],
            dst_ref=gb.at[rows(2 * i + c)],
            send_sem=gx_send.at[i],
            recv_sem=gx_recv.at[i],
            device_id=other,
            device_id_type=MESH,
        )

    def to_owner(i, source, target, sends, recvs):
        return pltpu.make_async_remote_copy(
            src_ref=source,
            dst_ref=target.at[0, :, head(mine)],
            send_sem=sends.at[i],
            recv_sem=recvs.at[mine],
            device_id={"tm": 2 * i + c},
            device_id_type=MESH,
        )

    def hand_over(i, source, target, sends, recvs):
        @pl.when(x != i)
        def _():
            to_owner(i, source, target, sends, recvs).start()

        @pl.when(x == i)
        def _():
            pltpu.make_async_copy(source, target.at[0, :, head(mine)], recvs.at[mine]).start()

    def generated(i):
        return gb.at[rows(2 * i + c)]

    def scored(i):
        return sb.at[pl.ds(i * TOK, TOK)]

    def attend(queries, keys, values, tiles, bias):
        top = [None, None]
        for t in tiles:
            s = lax.dot_general(
                queries, keys[t * 256 : t * 256 + 256, :], (((1,), (1,)), ((), ())),
                preferred_element_type=jnp.float32,
            )
            for r in range(2):
                for u in range(2):
                    piece = s[r * TOK : r * TOK + TOK, u * TOK : u * TOK + TOK] + bias(r, 2 * t + u)
                    scores[r * TOK : r * TOK + TOK, (2 * t + u) * TOK : (2 * t + u + 1) * TOK] = piece
                    top[r] = piece if top[r] is None else jnp.maximum(top[r], piece)
        peak = jnp.concatenate([jnp.max(top[r], axis=1, keepdims=True) for r in range(2)], axis=0)
        total = jnp.zeros((2 * TOK, TOK), jnp.float32)
        acc = jnp.zeros((2 * TOK, HD), jnp.float32)
        for t in tiles:
            p = jnp.exp2((scores[:, t * 256 : t * 256 + 256] - peak) * FACTOR)
            total = total + (p[:, :TOK] + p[:, TOK:])
            acc = acc + jnp.dot(
                p.astype(jnp.bfloat16), values[t * 256 : t * 256 + 256, :],
                preferred_element_type=jnp.float32,
            )
        return acc / jnp.sum(total, axis=1, keepdims=True)

    @pl.when(active)
    def _():
        for d in ORDER:
            chip = lax.rem(x + d, CHIPS)
            for a in (K, Q, V):
                arrived(a, chip)
                if a in RELAYED:
                    relay(a, chip).start()
        for chip in range(CHIPS):
            relayed(K, chip)
            relayed(V, chip)

        @pl.when(early)
        def _():
            pl.semaphore_wait(ready, len(IDLE))

        first = stagger[0]
        for p in range(4):
            def student_bias(r, j):
                own = 2 * (2 * p + r) + c
                allowed = (j == own) | ((j >= first) & (j < own))
                return jnp.where(allowed, 0.0, NEG).astype(jnp.float32)

            mixed = attend(qb[p * 256 : p * 256 + 256, :], kb, vb, range(2 * p + 2), student_bias)
            mixed = mixed.astype(jnp.bfloat16)
            for r in range(2):
                gb[rows(2 * (2 * p + r) + c), :] = mixed[r * TOK : r * TOK + TOK, :]
            if p > 0:
                for i in (2 * p - 2, 2 * p - 1):
                    to_other(i).start()
                    hand_over(i, generated(i), gen, go_send, go_recv)

        for d in ORDER:
            chip = lax.rem(x + d, CHIPS)
            arrived(TQ, chip)
            arrived(TK, chip)
            relay(TK, chip).start()
            if d == 0:
                for i in (6, 7):
                    to_other(i).start()
                    hand_over(i, generated(i), gen, go_send, go_recv)
        for chip in range(CHIPS):
            relayed(TK, chip)
        for i in range(CHIPS):
            pltpu.make_async_copy(gb.at[rows(2 * i + 1 - c)], gb.at[rows(2 * i + 1 - c)], gx_recv.at[i]).wait()

        ends = [clips[0, 0], clips[0, 0] + clips[0, 1]]

        def clip_of(block):
            return (ends[0] <= block).astype(jnp.int32) + (ends[1] <= block).astype(jnp.int32)

        for p in (0, 3, 1, 2):
            def teacher_bias(r, j):
                same = clip_of(2 * (2 * p + r) + c) == clip_of(jnp.int32(j))
                return jnp.where(same, 0.0, NEG).astype(jnp.float32)

            tiles = range(max(0, 2 * p - 4), min(8, 2 * p + 6))
            mixed = attend(tqb[p * 256 : p * 256 + 256, :], tkb, gb, tiles, teacher_bias)
            for r in range(2):
                i = 2 * p + r
                own = gb[rows(2 * i + c), :].astype(jnp.float32)
                sb[i * TOK : i * TOK + TOK, :] = (mixed[r * TOK : r * TOK + TOK, :] - own).astype(jnp.bfloat16)
            for i in (2 * p, 2 * p + 1):
                hand_over(i, scored(i), score, so_send, so_recv)

        for chip in range(CHIPS):
            for a in RELAYED:
                relay(a, chip).wait_send()
            to_other(chip).wait_send()

            @pl.when(x != chip)
            def _():
                to_owner(chip, generated(chip), gen, go_send, go_recv).wait_send()
                to_owner(chip, scored(chip), score, so_send, so_recv).wait_send()

    for a in range(5):
        for h in range(HEADS):
            @pl.when(x != HOME[h])
            def _():
                outgoing(a, h).wait_send()

    for target, recvs in ((gen, go_recv), (score, so_recv)):
        for h in range(HEADS):
            spot = target.at[0, :, pl.ds(h * HD, HD)]
            pltpu.make_async_copy(spot, spot, recvs.at[h]).wait()


def settle(a, b, c, d, sems):
    one = pltpu.make_async_copy(a, c, sems.at[0])
    two = pltpu.make_async_copy(b, d, sems.at[1])
    one.start()
    two.start()
    one.wait()
    two.wait()


def per_device(student_q, student_k, student_v, teacher_q, teacher_k, stagger, clip_lengths):
    whole = jax.ShapeDtypeStruct(student_q.shape, jnp.bfloat16)
    anywhere = pl.BlockSpec(memory_space=pl.ANY)
    scalars = pl.BlockSpec(memory_space=pltpu.SMEM)
    half, full = (BLOCKS // 2 * TOK, HD), (BLOCKS * TOK, HD)
    dma = pltpu.SemaphoreType.DMA
    outs = pl.pallas_call(
        kernel,
        out_shape=(whole, whole),
        in_specs=[anywhere] * 5 + [scalars] * 2,
        out_specs=(anywhere, anywhere),
        scratch_shapes=[
            pltpu.VMEM(half, jnp.bfloat16),
            pltpu.VMEM(full, jnp.bfloat16),
            pltpu.VMEM(full, jnp.bfloat16),
            pltpu.VMEM(half, jnp.bfloat16),
            pltpu.VMEM(full, jnp.bfloat16),
            pltpu.VMEM(full, jnp.bfloat16),
            pltpu.VMEM(half, jnp.bfloat16),
            pltpu.VMEM((2 * TOK, BLOCKS * TOK), jnp.float32),
            dma((5, HEADS)),
            dma((5, CHIPS)),
            dma((3, CHIPS)),
            dma((3, CHIPS)),
            dma((CHIPS,)),
            dma((CHIPS,)),
            dma((CHIPS,)),
            dma((HEADS,)),
            dma((CHIPS,)),
            dma((HEADS,)),
            pltpu.SemaphoreType.REGULAR,
            pltpu.SemaphoreType.REGULAR,
        ],
        compiler_params=pltpu.CompilerParams(collective_id=0, has_side_effects=True),
        name="rollout",
    )(student_q, student_k, student_v, teacher_q, teacher_k, stagger, clip_lengths)
    return pl.pallas_call(
        settle,
        out_shape=(whole, whole),
        in_specs=[pl.BlockSpec(memory_space=pltpu.VMEM)] * 2,
        out_specs=(anywhere, anywhere),
        scratch_shapes=[dma((2,))],
        name="settle",
    )(*outs)


def solution(mesh):
    rows = P("seq", "tm", "mp")
    return jax.shard_map(
        per_device,
        mesh=mesh,
        in_specs=(rows,) * 5 + (P("seq"), P("seq", None)),
        out_specs=(rows, rows),
        check_vma=False,
    )
```

```python
import math

import jax
import jax.numpy as jnp
from jax import lax
from jax.experimental import pallas as pl
from jax.experimental.pallas import tpu as pltpu
from jax.sharding import PartitionSpec as P

HD = 128
TOK = 128
CHIPS = 8
HEADS = 5
BLOCKS = 16
MESH = pl.DeviceIdType.MESH
NEG = -1e30
FACTOR = math.log2(math.e) / math.sqrt(HD)
HOME = (0, 2, 3, 5, 6)
LATE = ((0,), (3, 5))
IDLE = tuple(chip for chip in range(CHIPS) if chip not in HOME)
ORDER = (0, 1, 7, 2, 6, 3, 5, 4)

Q, K, V, TQ, TK = range(5)
RELAYED = (K, V, TK)


def kernel(
    sq, sk, sv, tq, tk, stagger, clips, gen, score,
    qb, kb, vb, tqb, tkb, gb, sb, scores,
    send, recv, rel_send, rel_recv, gx_send, gx_recv, go_send, go_recv, so_send, so_recv, ready, settled, paired,
):
    me = lax.axis_index("tm")
    x = me // 2
    c = lax.rem(me, 2)
    mine = sum(h * (x == HOME[h]).astype(jnp.int32) for h in range(HEADS))
    corner = (lax.axis_index("seq") == 0) & (lax.axis_index("mp") == 0)

    def late(h):
        return (corner & (HOME[h] in LATE[0])) | (jnp.logical_not(corner) & (HOME[h] in LATE[1]))

    lates = jnp.where(corner, len(LATE[0]), len(LATE[1]))
    active = x == HOME[0]
    last = (x == HOME[0]) & late(0)
    for h in range(1, HEADS):
        active = active | (x == HOME[h])
        last = last | ((x == HOME[h]) & late(h))
    inputs = (sq, sk, sv, tq, tk)
    buffers = (qb, kb, vb, tqb, tkb)
    other = {"tm": 2 * x + 1 - c}

    def rows(block):
        return pl.ds(pl.multiple_of(block * TOK, TOK), TOK)

    def head(h):
        return pl.ds(pl.multiple_of(h * HD, HD), HD)

    def place(a, chip, core):
        return buffers[a].at[rows(chip) if a in (Q, TQ) else rows(2 * chip + core)]

    barrier = pltpu.get_barrier_semaphore()
    early = active & jnp.logical_not(last)

    def greet(chip):
        pl.semaphore_signal(barrier, inc=1, device_id={"tm": 2 * chip + c}, device_id_type=MESH)

    @pl.when(early)
    def _():
        for d in ORDER[1:]:
            greet(lax.rem(x + d, CHIPS))

    @pl.when(jnp.logical_not(early))
    def _():
        for h in range(HEADS):
            @pl.when((x != HOME[h]) & late(h))
            def _():
                greet(HOME[h])

    @pl.when(active & (c == 1))
    def _():
        pl.semaphore_signal(barrier, inc=1, device_id=other, device_id_type=MESH)

    pairing = (active & (c == 0)).astype(jnp.int32)
    pl.semaphore_wait(barrier, jnp.where(last, CHIPS - 1, HEADS - lates - early.astype(jnp.int32)) + pairing)

    @pl.when(active & (c == 0))
    def _():
        pl.semaphore_signal(paired, inc=1, device_id=other, device_id_type=MESH)

    @pl.when(last)
    def _():
        for chip in IDLE:
            pl.semaphore_signal(settled, inc=1, device_id={"tm": 2 * chip + c}, device_id_type=MESH)
        for h in range(HEADS):
            @pl.when(jnp.logical_not(late(h)))
            def _():
                pl.semaphore_signal(settled, inc=1, device_id={"tm": 2 * HOME[h] + c}, device_id_type=MESH)

    def outgoing(a, h):
        return pltpu.make_async_remote_copy(
            src_ref=inputs[a].at[0, :, pl.ds(h * HD, HD)],
            dst_ref=place(a, x, c),
            send_sem=send.at[a, h],
            recv_sem=recv.at[a, x],
            device_id={"tm": 2 * HOME[h] + c},
            device_id_type=MESH,
        )

    def submit(arrays, chosen):
        for a in arrays:
            for h in range(HEADS):
                @pl.when((x != HOME[h]) & chosen(h))
                def _():
                    outgoing(a, h).start()

                @pl.when((x == HOME[h]) & chosen(h))
                def _():
                    pltpu.make_async_copy(
                        inputs[a].at[0, :, pl.ds(h * HD, HD)], place(a, x, c), recv.at[a, x]
                    ).start()

    submit((K, Q, V), lambda h: jnp.logical_not(late(h)))

    @pl.when(jnp.logical_not(active))
    def _():
        for h in range(HEADS):
            @pl.when(jnp.logical_not(late(h)))
            def _():
                pl.semaphore_signal(ready, inc=1, device_id={"tm": 2 * HOME[h] + c}, device_id_type=MESH)

    @pl.when(jnp.logical_not(last))
    def _():
        pl.semaphore_wait(settled, lates)

    submit((K, Q, V), late)
    submit((TQ, TK), lambda h: True)

    def arrived(a, chip):
        pltpu.make_async_copy(place(a, chip, c), place(a, chip, c), recv.at[a, chip]).wait()

    def relay(a, chip):
        r = RELAYED.index(a)
        return pltpu.make_async_remote_copy(
            src_ref=place(a, chip, c),
            dst_ref=place(a, chip, c),
            send_sem=rel_send.at[r, chip],
            recv_sem=rel_recv.at[r, chip],
            device_id=other,
            device_id_type=MESH,
        )

    def relayed(a, chip):
        r = RELAYED.index(a)
        pltpu.make_async_copy(place(a, chip, 1 - c), place(a, chip, 1 - c), rel_recv.at[r, chip]).wait()

    def to_other(i):
        return pltpu.make_async_remote_copy(
            src_ref=gb.at[rows(2 * i + c)],
            dst_ref=gb.at[rows(2 * i + c)],
            send_sem=gx_send.at[i],
            recv_sem=gx_recv.at[i],
            device_id=other,
            device_id_type=MESH,
        )

    def to_owner(i, source, target, sends, recvs):
        return pltpu.make_async_remote_copy(
            src_ref=source,
            dst_ref=target.at[0, :, head(mine)],
            send_sem=sends.at[i],
            recv_sem=recvs.at[mine],
            device_id={"tm": 2 * i + c},
            device_id_type=MESH,
        )

    def hand_over(i, source, target, sends, recvs):
        @pl.when(x != i)
        def _():
            to_owner(i, source, target, sends, recvs).start()

        @pl.when(x == i)
        def _():
            pltpu.make_async_copy(source, target.at[0, :, head(mine)], recvs.at[mine]).start()

    def generated(i):
        return gb.at[rows(2 * i + c)]

    def scored(i):
        return sb.at[pl.ds(i * TOK, TOK)]

    def attend(queries, keys, values, tiles, bias):
        top = [None, None]
        for t in tiles:
            s = lax.dot_general(
                queries, keys[t * 256 : t * 256 + 256, :], (((1,), (1,)), ((), ())),
                preferred_element_type=jnp.float32,
            )
            for r in range(2):
                for u in range(2):
                    piece = s[r * TOK : r * TOK + TOK, u * TOK : u * TOK + TOK] + bias(r, 2 * t + u)
                    scores[r * TOK : r * TOK + TOK, (2 * t + u) * TOK : (2 * t + u + 1) * TOK] = piece
                    top[r] = piece if top[r] is None else jnp.maximum(top[r], piece)
        peak = jnp.concatenate([jnp.max(top[r], axis=1, keepdims=True) for r in range(2)], axis=0)
        total = jnp.zeros((2 * TOK, TOK), jnp.float32)
        acc = jnp.zeros((2 * TOK, HD), jnp.float32)
        for t in tiles:
            p = jnp.exp2((scores[:, t * 256 : t * 256 + 256] - peak) * FACTOR)
            total = total + (p[:, :TOK] + p[:, TOK:])
            acc = acc + jnp.dot(
                p.astype(jnp.bfloat16), values[t * 256 : t * 256 + 256, :],
                preferred_element_type=jnp.float32,
            )
        return acc / jnp.sum(total, axis=1, keepdims=True)

    @pl.when(active)
    def _():
        @pl.when(c == 1)
        def _():
            pl.semaphore_wait(paired, 1)

        for d in ORDER:
            chip = lax.rem(x + d, CHIPS)
            for a in (K, Q, V):
                arrived(a, chip)
                if a in RELAYED:
                    relay(a, chip).start()
        for chip in range(CHIPS):
            relayed(K, chip)
            relayed(V, chip)

        @pl.when(early)
        def _():
            pl.semaphore_wait(ready, len(IDLE))

        first = stagger[0]
        for p in range(4):
            def student_bias(r, j):
                own = 2 * (2 * p + r) + c
                allowed = (j == own) | ((j >= first) & (j < own))
                return jnp.where(allowed, 0.0, NEG).astype(jnp.float32)

            mixed = attend(qb[p * 256 : p * 256 + 256, :], kb, vb, range(2 * p + 2), student_bias)
            mixed = mixed.astype(jnp.bfloat16)
            for r in range(2):
                gb[rows(2 * (2 * p + r) + c), :] = mixed[r * TOK : r * TOK + TOK, :]
            if p > 0:
                for i in (2 * p - 2, 2 * p - 1):
                    to_other(i).start()
                    hand_over(i, generated(i), gen, go_send, go_recv)

        for d in ORDER:
            chip = lax.rem(x + d, CHIPS)
            arrived(TQ, chip)
            arrived(TK, chip)
            relay(TK, chip).start()
            if d == 0:
                for i in (6, 7):
                    to_other(i).start()
                    hand_over(i, generated(i), gen, go_send, go_recv)
        for chip in range(CHIPS):
            relayed(TK, chip)
        for i in range(CHIPS):
            pltpu.make_async_copy(gb.at[rows(2 * i + 1 - c)], gb.at[rows(2 * i + 1 - c)], gx_recv.at[i]).wait()

        ends = [clips[0, 0], clips[0, 0] + clips[0, 1]]

        def clip_of(block):
            return (ends[0] <= block).astype(jnp.int32) + (ends[1] <= block).astype(jnp.int32)

        for p in (0, 3, 1, 2):
            def teacher_bias(r, j):
                same = clip_of(2 * (2 * p + r) + c) == clip_of(jnp.int32(j))
                return jnp.where(same, 0.0, NEG).astype(jnp.float32)

            tiles = range(max(0, 2 * p - 4), min(8, 2 * p + 6))
            mixed = attend(tqb[p * 256 : p * 256 + 256, :], tkb, gb, tiles, teacher_bias)
            for r in range(2):
                i = 2 * p + r
                own = gb[rows(2 * i + c), :].astype(jnp.float32)
                sb[i * TOK : i * TOK + TOK, :] = (mixed[r * TOK : r * TOK + TOK, :] - own).astype(jnp.bfloat16)
            for i in (2 * p, 2 * p + 1):
                hand_over(i, scored(i), score, so_send, so_recv)

        for chip in range(CHIPS):
            for a in RELAYED:
                relay(a, chip).wait_send()
            to_other(chip).wait_send()

            @pl.when(x != chip)
            def _():
                to_owner(chip, generated(chip), gen, go_send, go_recv).wait_send()
                to_owner(chip, scored(chip), score, so_send, so_recv).wait_send()

    for a in range(5):
        for h in range(HEADS):
            @pl.when(x != HOME[h])
            def _():
                outgoing(a, h).wait_send()

    for target, recvs in ((gen, go_recv), (score, so_recv)):
        for h in range(HEADS):
            spot = target.at[0, :, pl.ds(h * HD, HD)]
            pltpu.make_async_copy(spot, spot, recvs.at[h]).wait()


def settle(a, b, c, d, sems):
    one = pltpu.make_async_copy(a, c, sems.at[0])
    two = pltpu.make_async_copy(b, d, sems.at[1])
    one.start()
    two.start()
    one.wait()
    two.wait()


def per_device(student_q, student_k, student_v, teacher_q, teacher_k, stagger, clip_lengths):
    whole = jax.ShapeDtypeStruct(student_q.shape, jnp.bfloat16)
    anywhere = pl.BlockSpec(memory_space=pl.ANY)
    scalars = pl.BlockSpec(memory_space=pltpu.SMEM)
    half, full = (BLOCKS // 2 * TOK, HD), (BLOCKS * TOK, HD)
    dma = pltpu.SemaphoreType.DMA
    outs = pl.pallas_call(
        kernel,
        out_shape=(whole, whole),
        in_specs=[anywhere] * 5 + [scalars] * 2,
        out_specs=(anywhere, anywhere),
        scratch_shapes=[
            pltpu.VMEM(half, jnp.bfloat16),
            pltpu.VMEM(full, jnp.bfloat16),
            pltpu.VMEM(full, jnp.bfloat16),
            pltpu.VMEM(half, jnp.bfloat16),
            pltpu.VMEM(full, jnp.bfloat16),
            pltpu.VMEM(full, jnp.bfloat16),
            pltpu.VMEM(half, jnp.bfloat16),
            pltpu.VMEM((2 * TOK, BLOCKS * TOK), jnp.float32),
            dma((5, HEADS)),
            dma((5, CHIPS)),
            dma((3, CHIPS)),
            dma((3, CHIPS)),
            dma((CHIPS,)),
            dma((CHIPS,)),
            dma((CHIPS,)),
            dma((HEADS,)),
            dma((CHIPS,)),
            dma((HEADS,)),
            pltpu.SemaphoreType.REGULAR,
            pltpu.SemaphoreType.REGULAR,
            pltpu.SemaphoreType.REGULAR,
        ],
        compiler_params=pltpu.CompilerParams(collective_id=0, has_side_effects=True),
        name="rollout",
    )(student_q, student_k, student_v, teacher_q, teacher_k, stagger, clip_lengths)
    return pl.pallas_call(
        settle,
        out_shape=(whole, whole),
        in_specs=[pl.BlockSpec(memory_space=pltpu.VMEM)] * 2,
        out_specs=(anywhere, anywhere),
        scratch_shapes=[dma((2,))],
        name="settle",
    )(*outs)


def solution(mesh):
    rows = P("seq", "tm", "mp")
    return jax.shard_map(
        per_device,
        mesh=mesh,
        in_specs=(rows,) * 5 + (P("seq"), P("seq", None)),
        out_specs=(rows, rows),
        check_vma=False,
    )
```

```python
import math

import jax
import jax.numpy as jnp
from jax import lax
from jax.experimental import pallas as pl
from jax.experimental.pallas import tpu as pltpu
from jax.sharding import PartitionSpec as P

HD = 128
TOK = 128
CHIPS = 8
HEADS = 5
BLOCKS = 16
MESH = pl.DeviceIdType.MESH
NEG = -1e30
FACTOR = math.log2(math.e) / math.sqrt(HD)
HOME = (0, 2, 3, 5, 6)
LATE = ((0,), (3, 5))
IDLE = tuple(chip for chip in range(CHIPS) if chip not in HOME)
ORDER = (0, 1, 7, 2, 6, 3, 5, 4)

Q, K, V, TQ, TK = range(5)
RELAYED = (K, V, TK)


def kernel(
    sq, sk, sv, tq, tk, stagger, clips, gen, score,
    qb, kb, vb, tqb, tkb, gb, sb, scores,
    send, recv, rel_send, rel_recv, gx_send, gx_recv, go_send, go_recv, so_send, so_recv, ready, settled, paired,
):
    me = lax.axis_index("tm")
    x = me // 2
    c = lax.rem(me, 2)
    mine = sum(h * (x == HOME[h]).astype(jnp.int32) for h in range(HEADS))
    corner = (lax.axis_index("seq") == 0) & (lax.axis_index("mp") == 0)

    def late(h):
        return (corner & (HOME[h] in LATE[0])) | (jnp.logical_not(corner) & (HOME[h] in LATE[1]))

    lates = jnp.where(corner, len(LATE[0]), len(LATE[1]))
    active = x == HOME[0]
    last = (x == HOME[0]) & late(0)
    for h in range(1, HEADS):
        active = active | (x == HOME[h])
        last = last | ((x == HOME[h]) & late(h))
    inputs = (sq, sk, sv, tq, tk)
    buffers = (qb, kb, vb, tqb, tkb)
    other = {"tm": 2 * x + 1 - c}

    def rows(block):
        return pl.ds(pl.multiple_of(block * TOK, TOK), TOK)

    def head(h):
        return pl.ds(pl.multiple_of(h * HD, HD), HD)

    def place(a, chip, core):
        return buffers[a].at[rows(chip) if a in (Q, TQ) else rows(2 * chip + core)]

    barrier = pltpu.get_barrier_semaphore()
    early = active & jnp.logical_not(last)

    def greet(chip):
        pl.semaphore_signal(barrier, inc=1, device_id={"tm": 2 * chip + c}, device_id_type=MESH)

    @pl.when(early)
    def _():
        for d in ORDER[1:]:
            greet(lax.rem(x + d, CHIPS))

    @pl.when(jnp.logical_not(early))
    def _():
        for h in range(HEADS):
            @pl.when((x != HOME[h]) & late(h))
            def _():
                greet(HOME[h])

    @pl.when(active & (c == 1))
    def _():
        pl.semaphore_signal(barrier, inc=1, device_id=other, device_id_type=MESH)

    pairing = (active & (c == 0)).astype(jnp.int32)
    pl.semaphore_wait(barrier, jnp.where(last, CHIPS - 1, HEADS - lates - early.astype(jnp.int32)) + pairing)

    @pl.when(active & (c == 0))
    def _():
        pl.semaphore_signal(paired, inc=1, device_id=other, device_id_type=MESH)

    @pl.when(last)
    def _():
        for chip in IDLE:
            pl.semaphore_signal(settled, inc=1, device_id={"tm": 2 * chip + c}, device_id_type=MESH)
        for h in range(HEADS):
            @pl.when(jnp.logical_not(late(h)))
            def _():
                pl.semaphore_signal(settled, inc=1, device_id={"tm": 2 * HOME[h] + c}, device_id_type=MESH)

    def outgoing(a, h):
        return pltpu.make_async_remote_copy(
            src_ref=inputs[a].at[0, :, pl.ds(h * HD, HD)],
            dst_ref=place(a, x, c),
            send_sem=send.at[a, h],
            recv_sem=recv.at[a, x],
            device_id={"tm": 2 * HOME[h] + c},
            device_id_type=MESH,
        )

    def submit(arrays, chosen):
        for a in arrays:
            for h in range(HEADS):
                @pl.when((x != HOME[h]) & chosen(h))
                def _():
                    outgoing(a, h).start()

                @pl.when((x == HOME[h]) & chosen(h))
                def _():
                    pltpu.make_async_copy(
                        inputs[a].at[0, :, pl.ds(h * HD, HD)], place(a, x, c), recv.at[a, x]
                    ).start()

    submit((K, Q, V), lambda h: jnp.logical_not(late(h)))

    @pl.when(jnp.logical_not(active))
    def _():
        for h in range(HEADS):
            @pl.when(jnp.logical_not(late(h)))
            def _():
                pl.semaphore_signal(ready, inc=1, device_id={"tm": 2 * HOME[h] + c}, device_id_type=MESH)

    @pl.when(jnp.logical_not(last))
    def _():
        pl.semaphore_wait(settled, lates)

    submit((K, Q, V), late)
    submit((TQ, TK), lambda h: True)

    def arrived(a, chip):
        pltpu.make_async_copy(place(a, chip, c), place(a, chip, c), recv.at[a, chip]).wait()

    def relay(a, chip):
        r = RELAYED.index(a)
        return pltpu.make_async_remote_copy(
            src_ref=place(a, chip, c),
            dst_ref=place(a, chip, c),
            send_sem=rel_send.at[r, chip],
            recv_sem=rel_recv.at[r, chip],
            device_id=other,
            device_id_type=MESH,
        )

    def relayed(a, chip):
        r = RELAYED.index(a)
        pltpu.make_async_copy(place(a, chip, 1 - c), place(a, chip, 1 - c), rel_recv.at[r, chip]).wait()

    def to_other(i):
        return pltpu.make_async_remote_copy(
            src_ref=gb.at[rows(2 * i + c)],
            dst_ref=gb.at[rows(2 * i + c)],
            send_sem=gx_send.at[i],
            recv_sem=gx_recv.at[i],
            device_id=other,
            device_id_type=MESH,
        )

    def to_owner(i, source, target, sends, recvs):
        return pltpu.make_async_remote_copy(
            src_ref=source,
            dst_ref=target.at[0, :, head(mine)],
            send_sem=sends.at[i],
            recv_sem=recvs.at[mine],
            device_id={"tm": 2 * i + c},
            device_id_type=MESH,
        )

    def hand_over(i, source, target, sends, recvs):
        @pl.when(x != i)
        def _():
            to_owner(i, source, target, sends, recvs).start()

        @pl.when(x == i)
        def _():
            pltpu.make_async_copy(source, target.at[0, :, head(mine)], recvs.at[mine]).start()

    def generated(i):
        return gb.at[rows(2 * i + c)]

    def scored(i):
        return sb.at[pl.ds(i * TOK, TOK)]

    def attend(queries, keys, values, tiles, bias):
        top = [None, None]
        for t in tiles:
            s = lax.dot_general(
                queries, keys[t * 256 : t * 256 + 256, :], (((1,), (1,)), ((), ())),
                preferred_element_type=jnp.float32,
            )
            for r in range(2):
                for u in range(2):
                    piece = s[r * TOK : r * TOK + TOK, u * TOK : u * TOK + TOK] + bias(r, 2 * t + u)
                    scores[r * TOK : r * TOK + TOK, (2 * t + u) * TOK : (2 * t + u + 1) * TOK] = piece
                    top[r] = piece if top[r] is None else jnp.maximum(top[r], piece)
        peak = jnp.concatenate([jnp.max(top[r], axis=1, keepdims=True) for r in range(2)], axis=0)
        total = jnp.zeros((2 * TOK, TOK), jnp.float32)
        acc = jnp.zeros((2 * TOK, HD), jnp.float32)
        for t in tiles:
            p = jnp.exp2((scores[:, t * 256 : t * 256 + 256] - peak) * FACTOR)
            total = total + (p[:, :TOK] + p[:, TOK:])
            acc = acc + jnp.dot(
                p.astype(jnp.bfloat16), values[t * 256 : t * 256 + 256, :],
                preferred_element_type=jnp.float32,
            )
        return acc / jnp.sum(total, axis=1, keepdims=True)

    @pl.when(active)
    def _():
        @pl.when(c == 1)
        def _():
            pl.semaphore_wait(paired, 1)

        for d in ORDER:
            chip = lax.rem(x + d, CHIPS)
            for a in (K, Q, V):
                arrived(a, chip)
                if a in RELAYED:
                    relay(a, chip).start()
        for chip in range(CHIPS):
            relayed(K, chip)
            relayed(V, chip)

        @pl.when(early)
        def _():
            pl.semaphore_wait(ready, len(IDLE))

        first = stagger[0]
        for p in range(4):
            def student_bias(r, j):
                own = 2 * (2 * p + r) + c
                allowed = (j == own) | ((j >= first) & (j < own))
                return jnp.where(allowed, 0.0, NEG).astype(jnp.float32)

            mixed = attend(qb[p * 256 : p * 256 + 256, :], kb, vb, range(2 * p + 2), student_bias)
            mixed = mixed.astype(jnp.bfloat16)
            for r in range(2):
                gb[rows(2 * (2 * p + r) + c), :] = mixed[r * TOK : r * TOK + TOK, :]
            if p > 0:
                for i in (2 * p - 2, 2 * p - 1):
                    to_other(i).start()
                    hand_over(i, generated(i), gen, go_send, go_recv)

        for d in ORDER:
            chip = lax.rem(x + d, CHIPS)
            arrived(TQ, chip)
            arrived(TK, chip)
            relay(TK, chip).start()
            if d == 0:
                for i in (6, 7):
                    to_other(i).start()
                    hand_over(i, generated(i), gen, go_send, go_recv)
        for chip in range(CHIPS):
            relayed(TK, chip)
        for i in range(CHIPS):
            pltpu.make_async_copy(gb.at[rows(2 * i + 1 - c)], gb.at[rows(2 * i + 1 - c)], gx_recv.at[i]).wait()

        ends = [clips[0, 0], clips[0, 0] + clips[0, 1]]

        def clip_of(block):
            return (ends[0] <= block).astype(jnp.int32) + (ends[1] <= block).astype(jnp.int32)

        for p in (0, 3, 1, 2):
            def teacher_bias(r, j):
                same = clip_of(2 * (2 * p + r) + c) == clip_of(jnp.int32(j))
                return jnp.where(same, 0.0, NEG).astype(jnp.float32)

            tiles = range(max(0, 2 * p - 4), min(8, 2 * p + 6))
            mixed = attend(tqb[p * 256 : p * 256 + 256, :], tkb, gb, tiles, teacher_bias)
            for r in range(2):
                i = 2 * p + r
                own = gb[rows(2 * i + c), :].astype(jnp.float32)
                sb[i * TOK : i * TOK + TOK, :] = (mixed[r * TOK : r * TOK + TOK, :] - own).astype(jnp.bfloat16)
            for i in (2 * p, 2 * p + 1):
                hand_over(i, scored(i), score, so_send, so_recv)

        for chip in range(CHIPS):
            for a in RELAYED:
                relay(a, chip).wait_send()
            to_other(chip).wait_send()

            @pl.when(x != chip)
            def _():
                to_owner(chip, generated(chip), gen, go_send, go_recv).wait_send()
                to_owner(chip, scored(chip), score, so_send, so_recv).wait_send()

    for a in range(5):
        for h in range(HEADS):
            @pl.when(x != HOME[h])
            def _():
                outgoing(a, h).wait_send()

    for target, recvs in ((gen, go_recv), (score, so_recv)):
        for h in range(HEADS):
            spot = target.at[0, :, pl.ds(h * HD, HD)]
            pltpu.make_async_copy(spot, spot, recvs.at[h]).wait()


def settle(a, b, c, d, sems):
    one = pltpu.make_async_copy(a, c, sems.at[0])
    two = pltpu.make_async_copy(b, d, sems.at[1])
    one.start()
    two.start()
    one.wait()
    two.wait()


def per_device(student_q, student_k, student_v, teacher_q, teacher_k, stagger, clip_lengths):
    whole = jax.ShapeDtypeStruct(student_q.shape, jnp.bfloat16)
    anywhere = pl.BlockSpec(memory_space=pl.ANY)
    scalars = pl.BlockSpec(memory_space=pltpu.SMEM)
    half, full = (BLOCKS // 2 * TOK, HD), (BLOCKS * TOK, HD)
    dma = pltpu.SemaphoreType.DMA
    landing = pltpu.VMEM(student_q.shape, jnp.bfloat16)
    outs = pl.pallas_call(
        kernel,
        out_shape=(landing, landing),
        in_specs=[anywhere] * 5 + [scalars] * 2,
        out_specs=(pl.BlockSpec(memory_space=pltpu.VMEM),) * 2,
        scratch_shapes=[
            pltpu.VMEM(half, jnp.bfloat16),
            pltpu.VMEM(full, jnp.bfloat16),
            pltpu.VMEM(full, jnp.bfloat16),
            pltpu.VMEM(half, jnp.bfloat16),
            pltpu.VMEM(full, jnp.bfloat16),
            pltpu.VMEM(full, jnp.bfloat16),
            pltpu.VMEM(half, jnp.bfloat16),
            pltpu.VMEM((2 * TOK, BLOCKS * TOK), jnp.float32),
            dma((5, HEADS)),
            dma((5, CHIPS)),
            dma((3, CHIPS)),
            dma((3, CHIPS)),
            dma((CHIPS,)),
            dma((CHIPS,)),
            dma((CHIPS,)),
            dma((HEADS,)),
            dma((CHIPS,)),
            dma((HEADS,)),
            pltpu.SemaphoreType.REGULAR,
            pltpu.SemaphoreType.REGULAR,
            pltpu.SemaphoreType.REGULAR,
        ],
        compiler_params=pltpu.CompilerParams(collective_id=0, has_side_effects=True),
        name="rollout",
    )(student_q, student_k, student_v, teacher_q, teacher_k, stagger, clip_lengths)
    return pl.pallas_call(
        settle,
        out_shape=(whole, whole),
        in_specs=[pl.BlockSpec(memory_space=pltpu.VMEM)] * 2,
        out_specs=(anywhere, anywhere),
        scratch_shapes=[dma((2,))],
        name="settle",
    )(*[pltpu.with_memory_space_constraint(rows, pltpu.VMEM) for rows in outs])


def solution(mesh):
    rows = P("seq", "tm", "mp")
    return jax.shard_map(
        per_device,
        mesh=mesh,
        in_specs=(rows,) * 5 + (P("seq"), P("seq", None)),
        out_specs=(rows, rows),
        check_vma=False,
    )
```

```python
import math

import jax
import jax.numpy as jnp
from jax import lax
from jax.experimental import pallas as pl
from jax.experimental.pallas import tpu as pltpu
from jax.sharding import PartitionSpec as P

HD = 128
TOK = 128
CHIPS = 8
HEADS = 5
BLOCKS = 16
MESH = pl.DeviceIdType.MESH
NEG = -1e30
FACTOR = math.log2(math.e) / math.sqrt(HD)
HOME = (0, 2, 3, 5, 6)
LATE = ((0,), (3, 5))
IDLE = tuple(chip for chip in range(CHIPS) if chip not in HOME)
ORDER = (0, 1, 7, 2, 6, 3, 5, 4)

Q, K, V, TQ, TK = range(5)
RELAYED = (K, V, TK)


def kernel(
    sq, sk, sv, tq, tk, stagger, clips, gen, score,
    qb, kb, vb, tqb, tkb, gb, sb, scores,
    send, recv, rel_send, rel_recv, gx_send, gx_recv, go_send, go_recv, so_send, so_recv, ready, settled, paired,
):
    me = lax.axis_index("tm")
    x = me // 2
    c = lax.rem(me, 2)
    mine = sum(h * (x == HOME[h]).astype(jnp.int32) for h in range(HEADS))
    corner = (lax.axis_index("seq") == 0) & (lax.axis_index("mp") == 0)

    def late(chip):
        there, elsewhere = [chip == LATE[0][0], chip == LATE[1][0]]
        for other_chip in LATE[0][1:]:
            there = there | (chip == other_chip)
        for other_chip in LATE[1][1:]:
            elsewhere = elsewhere | (chip == other_chip)
        return (corner & there) | (jnp.logical_not(corner) & elsewhere)

    lates = jnp.where(corner, len(LATE[0]), len(LATE[1]))
    active = x == HOME[0]
    last = (x == HOME[0]) & late(HOME[0])
    for h in range(1, HEADS):
        active = active | (x == HOME[h])
        last = last | ((x == HOME[h]) & late(HOME[h]))
    inputs = (sq, sk, sv, tq, tk)
    buffers = (qb, kb, vb, tqb, tkb)
    other = {"tm": 2 * x + 1 - c}

    def rows(block):
        return pl.ds(pl.multiple_of(block * TOK, TOK), TOK)

    def head(h):
        return pl.ds(pl.multiple_of(h * HD, HD), HD)

    def place(a, chip, core):
        return buffers[a].at[rows(chip) if a in (Q, TQ) else rows(2 * chip + core)]

    barrier = pltpu.get_barrier_semaphore()
    early = active & jnp.logical_not(last)

    def greet(chip):
        pl.semaphore_signal(barrier, inc=1, device_id={"tm": 2 * chip + c}, device_id_type=MESH)

    @pl.when(early)
    def _():
        for d in ORDER[1:]:
            greet(lax.rem(x + d, CHIPS))

    @pl.when(jnp.logical_not(early))
    def _():
        for h in range(HEADS):
            @pl.when((x != HOME[h]) & late(HOME[h]))
            def _():
                greet(HOME[h])

    @pl.when(active & (c == 1))
    def _():
        pl.semaphore_signal(barrier, inc=1, device_id=other, device_id_type=MESH)

    pairing = (active & (c == 0)).astype(jnp.int32)
    pl.semaphore_wait(barrier, jnp.where(last, CHIPS - 1, HEADS - lates - early.astype(jnp.int32)) + pairing)

    @pl.when(active & (c == 0))
    def _():
        pl.semaphore_signal(paired, inc=1, device_id=other, device_id_type=MESH)

    @pl.when(last)
    def _():
        for chip in IDLE:
            pl.semaphore_signal(settled, inc=1, device_id={"tm": 2 * chip + c}, device_id_type=MESH)
        for h in range(HEADS):
            @pl.when(jnp.logical_not(late(HOME[h])))
            def _():
                pl.semaphore_signal(settled, inc=1, device_id={"tm": 2 * HOME[h] + c}, device_id_type=MESH)

    def outgoing(a, h, home):
        return pltpu.make_async_remote_copy(
            src_ref=inputs[a].at[0, :, head(h)],
            dst_ref=place(a, x, c),
            send_sem=send.at[a, h],
            recv_sem=recv.at[a, x],
            device_id={"tm": 2 * home + c},
            device_id_type=MESH,
        )

    far = (5 * lax.rem(x + 4, CHIPS) + 5) // CHIPS

    def submit(arrays, chosen):
        for a in arrays:
            for step in (0, 4, 1, 3, 2):
                h = lax.rem(far + step, HEADS)
                home = (CHIPS * h + 2) // HEADS

                @pl.when((x != home) & chosen(home))
                def _():
                    outgoing(a, h, home).start()

                @pl.when((x == home) & chosen(home))
                def _():
                    pltpu.make_async_copy(
                        inputs[a].at[0, :, head(h)], place(a, x, c), recv.at[a, x]
                    ).start()

    submit((K, Q, V), lambda home: jnp.logical_not(late(home)))

    @pl.when(jnp.logical_not(active))
    def _():
        for h in range(HEADS):
            @pl.when(jnp.logical_not(late(HOME[h])))
            def _():
                pl.semaphore_signal(ready, inc=1, device_id={"tm": 2 * HOME[h] + c}, device_id_type=MESH)

    @pl.when(jnp.logical_not(last))
    def _():
        pl.semaphore_wait(settled, lates)

    submit((K, Q, V), late)
    submit((TQ, TK), lambda home: True)

    def arrived(a, chip):
        pltpu.make_async_copy(place(a, chip, c), place(a, chip, c), recv.at[a, chip]).wait()

    def relay(a, chip):
        r = RELAYED.index(a)
        return pltpu.make_async_remote_copy(
            src_ref=place(a, chip, c),
            dst_ref=place(a, chip, c),
            send_sem=rel_send.at[r, chip],
            recv_sem=rel_recv.at[r, chip],
            device_id=other,
            device_id_type=MESH,
        )

    def relayed(a, chip):
        r = RELAYED.index(a)
        pltpu.make_async_copy(place(a, chip, 1 - c), place(a, chip, 1 - c), rel_recv.at[r, chip]).wait()

    def to_other(i):
        return pltpu.make_async_remote_copy(
            src_ref=gb.at[rows(2 * i + c)],
            dst_ref=gb.at[rows(2 * i + c)],
            send_sem=gx_send.at[i],
            recv_sem=gx_recv.at[i],
            device_id=other,
            device_id_type=MESH,
        )

    def to_owner(i, source, target, sends, recvs):
        return pltpu.make_async_remote_copy(
            src_ref=source,
            dst_ref=target.at[0, :, head(mine)],
            send_sem=sends.at[i],
            recv_sem=recvs.at[mine],
            device_id={"tm": 2 * i + c},
            device_id_type=MESH,
        )

    def hand_over(i, source, target, sends, recvs):
        @pl.when(x != i)
        def _():
            to_owner(i, source, target, sends, recvs).start()

        @pl.when(x == i)
        def _():
            pltpu.make_async_copy(source, target.at[0, :, head(mine)], recvs.at[mine]).start()

    def generated(i):
        return gb.at[rows(2 * i + c)]

    def scored(i):
        return sb.at[pl.ds(i * TOK, TOK)]

    def attend(queries, keys, values, tiles, bias):
        top = [None, None]
        for t in tiles:
            s = lax.dot_general(
                queries, keys[t * 256 : t * 256 + 256, :], (((1,), (1,)), ((), ())),
                preferred_element_type=jnp.float32,
            )
            for r in range(2):
                for u in range(2):
                    piece = s[r * TOK : r * TOK + TOK, u * TOK : u * TOK + TOK] + bias(r, 2 * t + u)
                    scores[r * TOK : r * TOK + TOK, (2 * t + u) * TOK : (2 * t + u + 1) * TOK] = piece
                    top[r] = piece if top[r] is None else jnp.maximum(top[r], piece)
        peak = jnp.concatenate([jnp.max(top[r], axis=1, keepdims=True) for r in range(2)], axis=0)
        total = jnp.zeros((2 * TOK, TOK), jnp.float32)
        acc = jnp.zeros((2 * TOK, HD), jnp.float32)
        for t in tiles:
            p = jnp.exp2((scores[:, t * 256 : t * 256 + 256] - peak) * FACTOR)
            total = total + (p[:, :TOK] + p[:, TOK:])
            acc = acc + jnp.dot(
                p.astype(jnp.bfloat16), values[t * 256 : t * 256 + 256, :],
                preferred_element_type=jnp.float32,
            )
        return acc / jnp.sum(total, axis=1, keepdims=True)

    @pl.when(active)
    def _():
        @pl.when(c == 1)
        def _():
            pl.semaphore_wait(paired, 1)

        for d in ORDER:
            chip = lax.rem(x + d, CHIPS)
            for a in (K, Q, V):
                arrived(a, chip)
                if a in RELAYED:
                    relay(a, chip).start()
        for chip in range(CHIPS):
            relayed(K, chip)
            relayed(V, chip)

        @pl.when(early)
        def _():
            pl.semaphore_wait(ready, len(IDLE))

        first = stagger[0]
        for p in range(4):
            def student_bias(r, j):
                own = 2 * (2 * p + r) + c
                allowed = (j == own) | ((j >= first) & (j < own))
                return jnp.where(allowed, 0.0, NEG).astype(jnp.float32)

            mixed = attend(qb[p * 256 : p * 256 + 256, :], kb, vb, range(2 * p + 2), student_bias)
            mixed = mixed.astype(jnp.bfloat16)
            for r in range(2):
                gb[rows(2 * (2 * p + r) + c), :] = mixed[r * TOK : r * TOK + TOK, :]
            if p > 0:
                for i in (2 * p - 2, 2 * p - 1):
                    to_other(i).start()
                    hand_over(i, generated(i), gen, go_send, go_recv)

        for d in ORDER:
            chip = lax.rem(x + d, CHIPS)
            arrived(TQ, chip)
            arrived(TK, chip)
            relay(TK, chip).start()
            if d == 0:
                for i in (6, 7):
                    to_other(i).start()
                    hand_over(i, generated(i), gen, go_send, go_recv)
        for chip in range(CHIPS):
            relayed(TK, chip)
        for i in range(CHIPS):
            pltpu.make_async_copy(gb.at[rows(2 * i + 1 - c)], gb.at[rows(2 * i + 1 - c)], gx_recv.at[i]).wait()

        ends = [clips[0, 0], clips[0, 0] + clips[0, 1]]

        def clip_of(block):
            return (ends[0] <= block).astype(jnp.int32) + (ends[1] <= block).astype(jnp.int32)

        for p in (0, 3, 1, 2):
            def teacher_bias(r, j):
                same = clip_of(2 * (2 * p + r) + c) == clip_of(jnp.int32(j))
                return jnp.where(same, 0.0, NEG).astype(jnp.float32)

            tiles = range(max(0, 2 * p - 4), min(8, 2 * p + 6))
            mixed = attend(tqb[p * 256 : p * 256 + 256, :], tkb, gb, tiles, teacher_bias)
            for r in range(2):
                i = 2 * p + r
                own = gb[rows(2 * i + c), :].astype(jnp.float32)
                sb[i * TOK : i * TOK + TOK, :] = (mixed[r * TOK : r * TOK + TOK, :] - own).astype(jnp.bfloat16)
            for i in (2 * p, 2 * p + 1):
                hand_over(i, scored(i), score, so_send, so_recv)

        for chip in range(CHIPS):
            for a in RELAYED:
                relay(a, chip).wait_send()
            to_other(chip).wait_send()

            @pl.when(x != chip)
            def _():
                to_owner(chip, generated(chip), gen, go_send, go_recv).wait_send()
                to_owner(chip, scored(chip), score, so_send, so_recv).wait_send()

    for a in range(5):
        for h in range(HEADS):
            @pl.when(x != HOME[h])
            def _():
                outgoing(a, h, HOME[h]).wait_send()

    for target, recvs in ((gen, go_recv), (score, so_recv)):
        for h in range(HEADS):
            spot = target.at[0, :, pl.ds(h * HD, HD)]
            pltpu.make_async_copy(spot, spot, recvs.at[h]).wait()


def settle(a, b, c, d, sems):
    one = pltpu.make_async_copy(a, c, sems.at[0])
    two = pltpu.make_async_copy(b, d, sems.at[1])
    one.start()
    two.start()
    one.wait()
    two.wait()


def per_device(student_q, student_k, student_v, teacher_q, teacher_k, stagger, clip_lengths):
    whole = jax.ShapeDtypeStruct(student_q.shape, jnp.bfloat16)
    anywhere = pl.BlockSpec(memory_space=pl.ANY)
    scalars = pl.BlockSpec(memory_space=pltpu.SMEM)
    half, full = (BLOCKS // 2 * TOK, HD), (BLOCKS * TOK, HD)
    dma = pltpu.SemaphoreType.DMA
    landing = pltpu.VMEM(student_q.shape, jnp.bfloat16)
    outs = pl.pallas_call(
        kernel,
        out_shape=(landing, landing),
        in_specs=[anywhere] * 5 + [scalars] * 2,
        out_specs=(pl.BlockSpec(memory_space=pltpu.VMEM),) * 2,
        scratch_shapes=[
            pltpu.VMEM(half, jnp.bfloat16),
            pltpu.VMEM(full, jnp.bfloat16),
            pltpu.VMEM(full, jnp.bfloat16),
            pltpu.VMEM(half, jnp.bfloat16),
            pltpu.VMEM(full, jnp.bfloat16),
            pltpu.VMEM(full, jnp.bfloat16),
            pltpu.VMEM(half, jnp.bfloat16),
            pltpu.VMEM((2 * TOK, BLOCKS * TOK), jnp.float32),
            dma((5, HEADS)),
            dma((5, CHIPS)),
            dma((3, CHIPS)),
            dma((3, CHIPS)),
            dma((CHIPS,)),
            dma((CHIPS,)),
            dma((CHIPS,)),
            dma((HEADS,)),
            dma((CHIPS,)),
            dma((HEADS,)),
            pltpu.SemaphoreType.REGULAR,
            pltpu.SemaphoreType.REGULAR,
            pltpu.SemaphoreType.REGULAR,
        ],
        compiler_params=pltpu.CompilerParams(collective_id=0, has_side_effects=True),
        name="rollout",
    )(student_q, student_k, student_v, teacher_q, teacher_k, stagger, clip_lengths)
    return pl.pallas_call(
        settle,
        out_shape=(whole, whole),
        in_specs=[pl.BlockSpec(memory_space=pltpu.VMEM)] * 2,
        out_specs=(anywhere, anywhere),
        scratch_shapes=[dma((2,))],
        name="settle",
    )(*[pltpu.with_memory_space_constraint(rows, pltpu.VMEM) for rows in outs])


def solution(mesh):
    rows = P("seq", "tm", "mp")
    return jax.shard_map(
        per_device,
        mesh=mesh,
        in_specs=(rows,) * 5 + (P("seq"), P("seq", None)),
        out_specs=(rows, rows),
        check_vma=False,
    )
```
